256 devices in a mesh: lat: 4 (over x_lo, core), lon: 64 (over x_hi, y, z).
Axes of the slice: x: 4 (x_hi: 2, x_lo: 2; x = x_hi * 2 + x_lo), y: 4, z: 8, core: 2. Of those that a mesh axis runs over, the one named last changes fastest.
Arguments:
- queries: bfloat16 [64, 1024, 1536], P('lat', 'lon'), may hold values from -12 to 12
- key_tokens: bfloat16 [64, 1024, 1536], P('lat', 'lon'), may hold values from -4 to 4
- value_tokens: bfloat16 [64, 1024, 1536], P('lat', 'lon'), may hold values from -6 to 6
- block_lists: int32 [8, 64, 8], P('lat', 'lon'), may hold values from 0 to 9, as said below
- band_rows: int32 [4, 1024], P('lat', 'lon'), may hold values from 0 to 255, as said below
Outputs:
- attended: bfloat16 [64, 1024, 1536], P('lat', 'lon')
The draws below stay inside these ranges and needn't reach their ends.
Inputs may be any that keep to these rules, and one draw needn't show every extreme that they name: `block_lists`: entry 0 of the list of query block b of a tile is its own block, 4 + b; the other entries are distinct candidate numbers, also distinct from entry 0. `band_rows`: the 16 token numbers of each tile are distinct.
All inputs are finite; a program needn't handle non-finite values.
Results may differ from the reference program's by a relative error of at most 0.0047.
Values may be sent and summed in bfloat16 or wider, within the bound.
No kernel may reach another device: no remote copies, remote signals or barrier semaphores. Data moves between devices by JAX's collectives and lax.ppermute only.
A program may use at most 128 MiB of HBM per device.

```python
import jax
import jax.numpy as jnp
from jax import lax

H = 24
HD = 64
D = 1536
BR = 8
BW = 16
BS = 128
LT = 2
NB = 8
PR = 16
CAND = 10
ROWS = 64
COLS = 1024
N_LAT = 4
N_LON = 64


def to_grid(blocked):
    split = blocked.reshape(N_LAT, LT, N_LON, BR, BW, D).transpose(0, 1, 3, 2, 4, 5)
    return split.reshape(ROWS, COLS, D)


def draw_key_tokens(key, part):
    own_key = jax.random.fold_in(key, 21)
    base_draw = jnp.clip(jax.random.normal(own_key, (N_LAT, LT, N_LON, BS, D), jnp.float32), -4.0, 4.0)
    return to_grid(base_draw).astype(jnp.bfloat16)


def draw_queries(key, part):
    own_key = jax.random.fold_in(key, 31)
    base_draw = jnp.clip(jax.random.normal(own_key, (N_LAT, LT, N_LON, BS, D), jnp.float32), -4.0, 4.0)
    return to_grid(base_draw).astype(jnp.bfloat16)


def draw_block_lists(key, part):
    own_key = jax.random.fold_in(key, 41)
    block_rows = LT * N_LAT
    ranks = jax.random.randint(own_key, (block_rows, N_LON, CAND), 0, 2 ** 16) * CAND + jnp.arange(CAND)[None, None, :]
    own_block = 2 * LT + jnp.arange(block_rows) % LT
    is_own = jnp.arange(CAND)[None, None, :] == own_block[:, None, None]
    ranks = jnp.where(is_own, -1, ranks)
    order = jnp.argsort(ranks, axis=-1)
    return order[:, :, :NB].astype(jnp.int32)


def draw_band_rows(key, part):
    own_key = jax.random.fold_in(key, 51)
    tile_size = LT * BS
    ranks = jax.random.randint(own_key, (N_LAT, N_LON, tile_size), 0, 2 ** 16) * tile_size + jnp.arange(tile_size)[None, None, :]
    order = jnp.argsort(ranks, axis=-1)
    return order[:, :, :PR].reshape(N_LAT, N_LON * PR).astype(jnp.int32)


def shard_levels(key, dims, cuts, least, largest):
    loudness, own = 1.0, jax.random.fold_in(key, 6)
    for position, parts in cuts:
        steps = jnp.exp(jax.random.uniform(jax.random.fold_in(own, position), (parts,), jnp.float32, least / len(cuts), largest / len(cuts)))
        loudness = loudness * jnp.repeat(steps, dims[position] // parts).reshape([-1 if axis == position else 1 for axis in range(len(dims))])
    return loudness


def bell_draw(stream_key, dims, width, limit, cuts=(), kind=jnp.bfloat16):
    entries = width * jax.random.normal(stream_key, dims, jnp.float32)
    if cuts:
        entries = entries * shard_levels(stream_key, dims, cuts, -0.22, 0.18)
    return jnp.clip(entries, -limit, limit).astype(kind)


def setup_inputs(seed: int = 0) -> dict:
    streams_of = jax.random.split(jax.random.key(seed), 6)
    return {
        "queries": draw_queries(jax.random.fold_in(streams_of[5], 71), 0),
        "key_tokens": draw_key_tokens(jax.random.fold_in(streams_of[5], 71), 0),
        "value_tokens": bell_draw(streams_of[2], (ROWS, COLS, D), 1.0, 6.0, ((0, 4), (1, 64))),
        "block_lists": draw_block_lists(jax.random.fold_in(streams_of[5], 71), 0),
        "band_rows": draw_band_rows(jax.random.fold_in(streams_of[5], 71), 0),
    }


def block_attention(q_rows, key_set, value_set, live_mask):
    count = q_rows.shape[0]
    q_heads = q_rows.reshape(count, H, HD).astype(jnp.float32)
    k_heads = key_set.reshape(key_set.shape[0], H, HD).astype(jnp.float32)
    v_heads = value_set.reshape(value_set.shape[0], H, HD).astype(jnp.float32)
    scores = jnp.einsum("qhd,khd->hqk", q_heads, k_heads) * (HD ** -0.5)
    scores = jnp.where(live_mask[None, None, :], scores, -jnp.inf)
    row_max = jnp.max(scores, axis=-1, keepdims=True)
    exp_scores = jnp.exp(scores - row_max)
    totals = jnp.sum(exp_scores, axis=-1)
    weights = exp_scores.astype(jnp.bfloat16)
    mixture = jnp.einsum("hqk,khd->qhd", weights.astype(jnp.float32), v_heads)
    mixture = mixture / jnp.transpose(totals)[:, :, None]
    return mixture.reshape(count, H * HD).astype(jnp.bfloat16)


def take_rows(tile, picks):
    return tile[picks]


def reference(queries, key_tokens, value_tokens, block_lists, band_rows):
    def tiles(source):
        grid = source.reshape(N_LAT, LT * BR, N_LON, BW, D).transpose(0, 2, 1, 3, 4)
        return grid.reshape(N_LAT, N_LON, LT, BS, D)

    q_tiles = tiles(queries)
    k_tiles = tiles(key_tokens)
    v_tiles = tiles(value_tokens)
    band_pick = band_rows.reshape(N_LAT, N_LON, PR)
    take_all = jax.vmap(jax.vmap(take_rows))
    band_keys = take_all(k_tiles.reshape(N_LAT, N_LON, LT * BS, D), band_pick).reshape(N_LAT, N_LON * PR, D)
    band_values = take_all(v_tiles.reshape(N_LAT, N_LON, LT * BS, D), band_pick).reshape(N_LAT, N_LON * PR, D)
    list_grid = block_lists.reshape(N_LAT, LT, N_LON, NB).transpose(0, 2, 1, 3)

    def device(dev_index):
        lat_at = dev_index // N_LON
        lon_at = dev_index % N_LON
        beside_all = (lon_at + jnp.arange(-2, 3, dtype=jnp.int32)) % N_LON
        cand_keys = k_tiles[lat_at, beside_all].reshape(CAND, BS, D)
        cand_values = v_tiles[lat_at, beside_all].reshape(CAND, BS, D)
        is_polar = (lat_at == 0) | (lat_at == N_LAT - 1)
        live_mask = jnp.concatenate([jnp.ones((NB * BS,), jnp.bool_), jnp.full((N_LON * PR,), is_polar)])

        def one_block(inputs):
            q_rows, listed = inputs
            key_set = jnp.concatenate([cand_keys[listed].reshape(NB * BS, D), band_keys[lat_at]], 0)
            value_set = jnp.concatenate([cand_values[listed].reshape(NB * BS, D), band_values[lat_at]], 0)
            return block_attention(q_rows, key_set, value_set, live_mask)

        return lax.map(one_block, (q_tiles[lat_at, lon_at], list_grid[lat_at, lon_at]))

    results = lax.map(device, jnp.arange(N_LAT * N_LON, dtype=jnp.int32))
    grid = results.reshape(N_LAT, N_LON, LT * BR, BW, D).transpose(0, 2, 1, 3, 4)
    return grid.reshape(ROWS, COLS, D)
```

```python
import functools

import jax
import jax.numpy as jnp
from jax import lax
from jax.experimental import pallas as pl
from jax.experimental.pallas import tpu as pltpu
from jax.sharding import PartitionSpec as P

H = 24
HD = 64
BS = 128
TILE = 256
D = 1536
PAIR = 2 * HD
NB = 8
CAND = 10
N_LON = 64
LOG2E = 1.4426950408889634
CHUNK_PAIRS = (3, 3, 3, 3)
POLAR_LATS = (0, 3)


def step_lon(value, steps):
    pairs = [(source, (source + steps) % N_LON) for source in range(N_LON)]
    return lax.ppermute(value, "lon", pairs)


def polar_move(value, target_of):
    pairs = [
        (lat * N_LON + source, lat * N_LON + target_of(source))
        for lat in POLAR_LATS
        for source in range(N_LON)
    ]
    return lax.ppermute(value, ("lat", "lon"), pairs)


def along_z(steps):
    return lambda lon: (lon & ~7) | ((lon + steps) & 7)


def along_y(steps):
    return lambda lon: (lon & ~24) | ((lon + 8 * steps) & 24)


def across_x(lon):
    return lon ^ 32


def gather_band(picked):
    near = jnp.stack([picked, polar_move(picked, along_z(1)), polar_move(picked, along_z(-1))])
    row = jnp.concatenate([near, polar_move(near, along_z(3)), polar_move(near[:2], along_z(-3))])
    row = row.reshape(-1, row.shape[-1])
    both = jnp.concatenate([row, polar_move(row, across_x)])
    return (
        both,
        polar_move(both, along_y(1)),
        polar_move(both, along_y(-1)),
        polar_move(both, along_y(2)),
    )


def attend(queries, keys, values):
    scores = lax.dot_general(
        queries, keys, (((1,), (1,)), ((), ())), preferred_element_type=jnp.float32
    )
    row_max = jnp.max(scores, axis=1, keepdims=True)
    weights = jnp.exp2((scores - row_max) * LOG2E).astype(jnp.bfloat16)
    wide = jnp.concatenate([values, jnp.ones_like(values)], 1)
    mixed = jnp.dot(weights, wide, preferred_element_type=jnp.float32)
    return mixed[:, :PAIR] / mixed[:, PAIR:]


def attention_kernel(lists_ref, polar_ref, *refs):
    q_ref, tiles = refs[0], refs[1:6]
    band_k, band_v = refs[6:10], refs[10:14]
    out_ref, k_all, v_all = refs[-3:]
    for at, tile in enumerate(tiles):
        for block in range(2):
            rows = pl.ds(block * BS, BS)
            k_all[2 * at + block] = tile[0, rows, :]
            v_all[2 * at + block] = tile[1, rows, :]
    low = lax.broadcasted_iota(jnp.int32, (BS, PAIR), 1) < HD

    def run(with_band):
        for block in range(2):
            rows = pl.ds(block * BS, BS)
            q = q_ref[rows, :] * jnp.bfloat16(HD ** -0.5)
            zero = jnp.zeros_like(q)
            stacked = jnp.concatenate([jnp.where(low, q, zero), jnp.where(low, zero, q)], 0)
            picks = [lists_ref[block * NB + j] for j in range(NB)]
            keys = [k_all[pick] for pick in picks]
            values = [v_all[pick] for pick in picks]
            if with_band:
                keys += [ref[...] for ref in band_k]
                values += [ref[...] for ref in band_v]
            mixed = attend(stacked, jnp.concatenate(keys, 0), jnp.concatenate(values, 0))
            out_ref[rows, :] = jnp.where(low, mixed[:BS], mixed[BS:]).astype(out_ref.dtype)

    @pl.when(polar_ref[0] == 1)
    def _():
        run(True)

    @pl.when(polar_ref[0] == 0)
    def _():
        run(False)


def chunk_attention(first, count, lists, polar, queries, tiles, band, out):
    def of_chunk(p, lists_ref, polar_ref):
        return 0, 0, p

    def of_whole(p, lists_ref, polar_ref):
        return 0, first + p

    def of_band_k(p, lists_ref, polar_ref):
        return 0, (first + p) * polar_ref[0]

    def of_band_v(p, lists_ref, polar_ref):
        return 0, (D // PAIR + first + p) * polar_ref[0]

    whole = pl.BlockSpec((TILE, PAIR), of_whole)
    in_specs = (
        [whole]
        + [pl.BlockSpec((2, TILE, PAIR), of_chunk)] * 5
        + [pl.BlockSpec((TILE, PAIR), of_band_k)] * 4
        + [pl.BlockSpec((TILE, PAIR), of_band_v)] * 4
    )
    args = [lists, polar, queries, *tiles, *band, *band]
    aliases = {}
    if out is not None:
        in_specs.append(pl.BlockSpec(memory_space=pl.ANY))
        aliases = {len(args): 0}
        args.append(out)
    return pl.pallas_call(
        attention_kernel,
        out_shape=jax.ShapeDtypeStruct((TILE, D), jnp.bfloat16),
        grid_spec=pltpu.PrefetchScalarGridSpec(
            num_scalar_prefetch=2,
            grid=(count,),
            in_specs=in_specs,
            out_specs=whole,
            scratch_shapes=[pltpu.VMEM((CAND, BS, PAIR), jnp.bfloat16)] * 2,
        ),
        input_output_aliases=aliases,
        compiler_params=pltpu.CompilerParams(vmem_limit_bytes=48 << 20),
        cost_estimate=pl.CostEstimate(
            flops=count * 4 * TILE * 2048 * PAIR * 2,
            transcendentals=count * 2 * TILE * 2048,
            bytes_accessed=count * 14 * TILE * PAIR * 2,
        ),
        name=f"attention_{first}",
    )(*args)


def local(queries, key_tokens, value_tokens, block_lists, band_rows):
    q_rows = queries.reshape(TILE, D)
    k_rows = key_tokens.reshape(TILE, D)
    v_rows = value_tokens.reshape(TILE, D)
    lists = block_lists.reshape(2 * NB)
    lat_at = lax.axis_index("lat")
    polar = ((lat_at == 0) | (lat_at == lax.axis_size("lat") - 1)).astype(jnp.int32).reshape(1)
    picked = jnp.concatenate([k_rows[band_rows[0]], v_rows[band_rows[0]]], 1)
    chunks, at = [], 0
    for count in CHUNK_PAIRS:
        part = slice(at * PAIR, (at + count) * PAIR)
        own = jnp.stack([k_rows[:, part], v_rows[:, part]])
        west_one, east_one = step_lon(own, 1), step_lon(own, -1)
        west_two, east_two = step_lon(west_one, 1), step_lon(east_one, -1)
        chunks.append((at, count, (west_two, west_one, own, east_one, east_two)))
        at += count
    band = gather_band(picked)
    out = None
    for first, count, tiles in chunks:
        out = chunk_attention(first, count, lists, polar, q_rows, tiles, band, out)
    return out.reshape(queries.shape)


def solution(mesh):
    return jax.shard_map(
        local,
        mesh=mesh,
        in_specs=(
            P("lat", "lon", None),
            P("lat", "lon", None),
            P("lat", "lon", None),
            P("lat", "lon", None),
            P("lat", "lon"),
        ),
        out_specs=P("lat", "lon", None),
        check_vma=False,
    )
```

```python
import jax
import jax.numpy as jnp
from jax import lax
from jax.experimental import pallas as pl
from jax.experimental.pallas import tpu as pltpu
from jax.sharding import PartitionSpec as P

H = 24
HD = 64
BS = 128
TILE = 256
D = 1536
PAIR = 2 * HD
NB = 8
CAND = 10
N_LON = 64
LOG2E = 1.4426950408889634
STEP = 2 * PAIR
POLAR_LATS = (0, 3)


def step_lon(value, steps):
    pairs = [(source, (source + steps) % N_LON) for source in range(N_LON)]
    return lax.ppermute(value, "lon", pairs)


def core_move(value, toward_polar):
    pairs = [
        (side, home) if toward_polar else (home, side)
        for polar_lat, side_lat in ((0, 1), (3, 2))
        for home, side in (
            (polar_lat * N_LON + lon, side_lat * N_LON + lon) for lon in range(N_LON)
        )
    ]
    return lax.ppermute(value, ("lat", "lon"), pairs)


def share(value, groups):
    copies = jnp.broadcast_to(value, (8,) + value.shape)
    got = lax.all_to_all(copies, "lon", 0, 0, axis_index_groups=groups)
    return got.reshape((-1,) + value.shape[1:])


Z_LINES = [[first + z for z in range(8)] for first in range(0, N_LON, 8)]


def move(value, target_of):
    return lax.ppermute(value, "lon", [(lon, target_of(lon)) for lon in range(N_LON)])


def along_y(steps):
    return lambda lon: (lon & ~24) | ((lon + 8 * steps) & 24)


def across_x(lon):
    return lon ^ 32


def attend(queries, keys, values):
    scores = lax.dot_general(
        queries, keys, (((1,), (1,)), ((), ())), preferred_element_type=jnp.float32
    )
    row_max = jnp.max(scores, axis=1, keepdims=True)
    weights = jnp.exp2((scores - row_max) * LOG2E).astype(jnp.bfloat16)
    wide = jnp.concatenate([values, jnp.ones_like(values)], 1)
    mixed = jnp.dot(weights, wide, preferred_element_type=jnp.float32)
    return mixed[:, :PAIR] / mixed[:, PAIR:]


def attention_kernel(lists_ref, polar_ref, *refs):
    q_ref, k_tiles, v_tiles = refs[0], refs[1:6], refs[6:11]
    band_k, band_v = refs[11:16], refs[16:21]
    out_ref, k_all, v_all = refs[21:]
    for at in range(5):
        for block in range(2):
            rows = pl.ds(block * BS, BS)
            k_all[2 * at + block] = k_tiles[at][rows, :]
            v_all[2 * at + block] = v_tiles[at][rows, :]
    low = lax.broadcasted_iota(jnp.int32, (BS, PAIR), 1) < HD

    def run(with_band):
        for part in range(STEP // PAIR):
            lanes = slice(part * PAIR, (part + 1) * PAIR)
            for block in range(2):
                rows = pl.ds(block * BS, BS)
                q = q_ref[rows, lanes] * jnp.bfloat16(HD ** -0.5)
                zero = jnp.zeros_like(q)
                stacked = jnp.concatenate([jnp.where(low, q, zero), jnp.where(low, zero, q)], 0)
                picks = [lists_ref[block * NB + j] for j in range(NB)]
                keys = [k_all[pick, :, lanes] for pick in picks]
                values = [v_all[pick, :, lanes] for pick in picks]
                if with_band:
                    keys += [ref[:, lanes] for ref in band_k]
                    values += [ref[:, lanes] for ref in band_v]
                mixed = attend(stacked, jnp.concatenate(keys, 0), jnp.concatenate(values, 0))
                out_ref[rows, lanes] = jnp.where(low, mixed[:BS], mixed[BS:]).astype(out_ref.dtype)

    @pl.when(polar_ref[0] == 1)
    def _():
        run(True)

    @pl.when(polar_ref[0] == 0)
    def _():
        run(False)


def attention(lists, polar, queries, keys, values, band_k, band_v):
    column = pl.BlockSpec((TILE, STEP), lambda p, lists_ref, polar_ref: (0, p))
    band = [
        pl.BlockSpec((part.shape[0], STEP), lambda p, lists_ref, polar_ref: (0, p * polar_ref[0]))
        for part in band_k
    ]
    return pl.pallas_call(
        attention_kernel,
        out_shape=jax.ShapeDtypeStruct((TILE, D), jnp.bfloat16),
        grid_spec=pltpu.PrefetchScalarGridSpec(
            num_scalar_prefetch=2,
            grid=(D // STEP,),
            in_specs=[column] * 11 + band * 2,
            out_specs=column,
            scratch_shapes=[pltpu.VMEM((10, BS, STEP), jnp.bfloat16)] * 2,
        ),
        compiler_params=pltpu.CompilerParams(vmem_limit_bytes=60 << 20),
        cost_estimate=pl.CostEstimate(
            flops=4 * TILE * 2048 * D, transcendentals=0, bytes_accessed=TILE * D * 30
        ),
        name="attention",
    )(lists, polar, queries, *keys, *values, *band_k, *band_v)


def local(queries, key_tokens, value_tokens, block_lists, band_rows):
    q = queries.reshape(TILE, D)
    k = key_tokens.reshape(TILE, D)
    v = value_tokens.reshape(TILE, D)
    lists = block_lists.reshape(2 * NB)
    lat_at = lax.axis_index("lat")
    is_polar = (lat_at == 0) | (lat_at == lax.axis_size("lat") - 1)
    polar = is_polar.astype(jnp.int32).reshape(1)
    fence = lax.optimization_barrier

    picked = jnp.where(is_polar, k[band_rows[0]], core_move(v[band_rows[0]], False))
    k_west, k_east = step_lon(k, 1), step_lon(k, -1)
    k_west, k_east, v_sent = fence((k_west, k_east, v))
    v_west, v_east = step_lon(v_sent, 1), step_lon(v_sent, -1)
    k_west, k_east, v_west, v_east = fence((k_west, k_east, v_west, v_east))
    k_west2, k_east2 = step_lon(k_west, 1), step_lon(k_east, -1)
    v_west, v_east, k_west2, k_east2 = fence((v_west, v_east, k_west2, k_east2))
    v_west2, v_east2 = step_lon(v_west, 1), step_lon(v_east, -1)

    line = share(picked, Z_LINES)
    both = jnp.concatenate([line, move(line, across_x)], 0)
    south, north = move(both, along_y(1)), move(both, along_y(-1))
    z_at = lax.axis_index("lon") & 7
    first = jnp.where(z_at == 0, north[:BS], south[:BS])
    second = jnp.where(z_at == 7, south[BS:], north[BS:])
    south2 = move(first, lambda lon: along_y(-1 if lon & 7 == 0 else 1)(lon))
    north2 = move(second, lambda lon: along_y(1 if lon & 7 == 7 else -1)(lon))
    band = [both, south, north, south2, north2]
    band_v = [core_move(part, True) for part in band]
    out = attention(
        lists,
        polar,
        q,
        (k_west2, k_west, k, k_east, k_east2),
        (v_west2, v_west, v, v_east, v_east2),
        band,
        band_v,
    )
    return out.reshape(queries.shape)


def solution(mesh):
    return jax.shard_map(
        local,
        mesh=mesh,
        in_specs=(
            P("lat", "lon", None),
            P("lat", "lon", None),
            P("lat", "lon", None),
            P("lat", "lon", None),
            P("lat", "lon"),
        ),
        out_specs=P("lat", "lon", None),
        check_vma=False,
    )
```

```python
import jax
import jax.numpy as jnp
from jax import lax
from jax.experimental import pallas as pl
from jax.experimental.pallas import tpu as pltpu
from jax.sharding import PartitionSpec as P

H = 24
HD = 64
BS = 128
TILE = 256
D = 1536
PAIR = 2 * HD
NB = 8
CAND = 10
N_LON = 64
LOG2E = 1.4426950408889634
STEP = 2 * PAIR
TOTALS = 32
POLAR_LATS = (0, 3)
POLAR_LATS = (0, 3)


def step_lon(value, steps):
    pairs = [(source, (source + steps) % N_LON) for source in range(N_LON)]
    return lax.ppermute(value, "lon", pairs)


def core_move(value, toward_polar):
    pairs = [
        (side, home) if toward_polar else (home, side)
        for polar_lat, side_lat in ((0, 1), (3, 2))
        for home, side in (
            (polar_lat * N_LON + lon, side_lat * N_LON + lon) for lon in range(N_LON)
        )
    ]
    return lax.ppermute(value, ("lat", "lon"), pairs)


def share(value, groups):
    copies = jnp.broadcast_to(value, (8,) + value.shape)
    got = lax.all_to_all(copies, "lon", 0, 0, axis_index_groups=groups)
    return got.reshape((-1,) + value.shape[1:])


Z_LINES = [[first + z for z in range(8)] for first in range(0, N_LON, 8)]


def move(value, target_of):
    return lax.ppermute(value, "lon", [(lon, target_of(lon)) for lon in range(N_LON)])


def polar_move(value, target_of):
    pairs = [
        (lat * N_LON + lon, lat * N_LON + target_of(lon))
        for lat in POLAR_LATS
        for lon in range(N_LON)
    ]
    return lax.ppermute(value, ("lat", "lon"), pairs)


def along_y(steps):
    return lambda lon: (lon & ~24) | ((lon + 8 * steps) & 24)


def across_x(lon):
    return lon ^ 32


def low_lanes():
    return lax.broadcasted_iota(jnp.int32, (BS, PAIR), 1) < HD


def attend(q, keys, values, low):
    q = q * jnp.bfloat16(HD ** -0.5)
    zero = jnp.zeros_like(q)
    stacked = jnp.concatenate([jnp.where(low, q, zero), jnp.where(low, zero, q)], 0)
    keys, values = jnp.concatenate(keys, 0), jnp.concatenate(values, 0)
    scores = lax.dot_general(
        stacked, keys, (((1,), (1,)), ((), ())), preferred_element_type=jnp.float32
    )
    row_max = jnp.max(scores, axis=1, keepdims=True)
    weights = jnp.exp2((scores - row_max) * LOG2E).astype(jnp.bfloat16)
    wide = jnp.concatenate([values, jnp.ones_like(values)], 1)
    mixed = jnp.dot(weights, wide, preferred_element_type=jnp.float32)
    acc = jnp.where(low, mixed[:BS, :PAIR], mixed[BS:, :PAIR])
    total = jnp.where(low, mixed[:BS, PAIR:], mixed[BS:, PAIR:])
    return acc, total, row_max


def pack(stat, head, total, row_max):
    lane = lax.broadcasted_iota(jnp.int32, (BS, PAIR), 1)
    stat = jnp.where(lane == head, row_max[:BS], stat)
    stat = jnp.where(lane == head + 1, row_max[BS:], stat)
    stat = jnp.where(lane == head + TOTALS, total[:, :1], stat)
    return jnp.where(lane == head + 1 + TOTALS, total[:, HD:HD + 1], stat)


def band_kernel(polar_ref, q_own, q_other, *refs):
    band_k, band_v = refs[0:5], refs[5:10]
    outs, stats = refs[10:12], refs[12:14]
    at = pl.program_id(0)

    @pl.when(polar_ref[0] == 1)
    def _():
        low = low_lanes()
        for q_ref, out_ref, stat_ref in zip((q_own, q_other), outs, stats):
            for block in range(2):
                rows = pl.ds(block * BS, BS)
                stat = jnp.where(at == 0, 0.0, stat_ref[rows, :])
                for part in range(STEP // PAIR):
                    lanes = slice(part * PAIR, (part + 1) * PAIR)
                    acc, total, row_max = attend(
                        q_ref[rows, lanes],
                        [ref[:, lanes] for ref in band_k],
                        [ref[:, lanes] for ref in band_v],
                        low,
                    )
                    out_ref[rows, lanes] = (acc / total).astype(out_ref.dtype)
                    stat = pack(stat, 2 * (at * (STEP // PAIR) + part), total, row_max)
                stat_ref[rows, :] = stat


def near_kernel(lists_ref, *refs):
    q_ref, k_tiles, v_tiles = refs[0], refs[1:6], refs[6:11]
    out_ref, stat_ref, k_all, v_all = refs[11:]
    at = pl.program_id(0)
    for tile in range(5):
        for block in range(2):
            rows = pl.ds(block * BS, BS)
            k_all[2 * tile + block] = k_tiles[tile][rows, :]
            v_all[2 * tile + block] = v_tiles[tile][rows, :]
    low = low_lanes()
    for block in range(2):
        rows = pl.ds(block * BS, BS)
        stat = jnp.where(at == 0, 0.0, stat_ref[rows, :])
        picks = [lists_ref[block * NB + j] for j in range(NB)]
        for part in range(STEP // PAIR):
            lanes = slice(part * PAIR, (part + 1) * PAIR)
            acc, total, row_max = attend(
                q_ref[rows, lanes],
                [k_all[pick, :, lanes] for pick in picks],
                [v_all[pick, :, lanes] for pick in picks],
                low,
            )
            out_ref[rows, lanes] = acc / total
            stat = pack(stat, 2 * (at * (STEP // PAIR) + part), total, row_max)
        stat_ref[rows, :] = stat


def spread(share, at):
    high = share.astype(jnp.bfloat16)
    rest = share - high.astype(jnp.float32)
    middle = rest.astype(jnp.bfloat16)
    tail = (rest - middle.astype(jnp.float32)).astype(jnp.bfloat16)
    column = lax.broadcasted_iota(jnp.int32, (PAIR, STEP), 0)
    lane = lax.broadcasted_iota(jnp.int32, (PAIR, STEP), 1)
    select = jnp.where(column == at * (STEP // HD) + lane // HD, 1.0, 0.0).astype(jnp.bfloat16)
    pieces = jnp.concatenate([high, middle, tail], 1)
    return jnp.dot(
        pieces, jnp.concatenate([select] * 3, 0), preferred_element_type=jnp.float32
    )


def merge_kernel(polar_ref, near_ref, own_ref, other_ref, *refs):
    stats, out_ref = refs[0:3], refs[3]
    at = pl.program_id(0)

    @pl.when(polar_ref[0] == 1)
    def _():
        heads = lax.broadcasted_iota(jnp.int32, (TILE, PAIR), 1) < D // HD
        stat = [ref[...] for ref in stats]
        top = jnp.maximum(stat[0], jnp.maximum(stat[1], stat[2]))
        masses = [
            jnp.exp2((each - top) * LOG2E) * pltpu.roll(each, PAIR - TOTALS, 1) for each in stat
        ]
        whole = masses[0] + masses[1] + masses[2]
        result = None
        for mass, ref in zip(masses, (near_ref, own_ref, other_ref)):
            share = jnp.where(heads, mass / whole, 0.0)
            part = ref[...].astype(jnp.float32) * spread(share, at)
            result = part if result is None else result + part
        out_ref[...] = result.astype(out_ref.dtype)

    @pl.when(polar_ref[0] == 0)
    def _():
        out_ref[...] = near_ref[...].astype(out_ref.dtype)


COLUMN = pl.BlockSpec((TILE, STEP), lambda p, *_: (0, p))
STAT = pl.BlockSpec((TILE, PAIR), lambda p, *_: (0, 0))
PARAMS = pltpu.CompilerParams(vmem_limit_bytes=60 << 20)


def band_attention(polar, q_own, q_other, band_k, band_v):
    def polar_column(rows):
        return pl.BlockSpec((rows, STEP), lambda p, polar_ref: (0, p * polar_ref[0]))

    return pl.pallas_call(
        band_kernel,
        out_shape=[jax.ShapeDtypeStruct((TILE, D), jnp.bfloat16)] * 2
        + [jax.ShapeDtypeStruct((TILE, PAIR), jnp.float32)] * 2,
        grid_spec=pltpu.PrefetchScalarGridSpec(
            num_scalar_prefetch=1,
            grid=(D // STEP,),
            in_specs=[polar_column(TILE)] * 2
            + [polar_column(part.shape[0]) for part in (*band_k, *band_v)],
            out_specs=[COLUMN] * 2 + [STAT] * 2,
        ),
        compiler_params=PARAMS,
        cost_estimate=pl.CostEstimate(
            flops=6 * 10 ** 10, transcendentals=0, bytes_accessed=TILE * D * 30
        ),
        name="band_attention",
    )(polar, q_own, q_other, *band_k, *band_v)


def near_attention(lists, queries, keys, values):
    return pl.pallas_call(
        near_kernel,
        out_shape=[
            jax.ShapeDtypeStruct((TILE, D), jnp.float32),
            jax.ShapeDtypeStruct((TILE, PAIR), jnp.float32),
        ],
        grid_spec=pltpu.PrefetchScalarGridSpec(
            num_scalar_prefetch=1,
            grid=(D // STEP,),
            in_specs=[COLUMN] * 11,
            out_specs=[COLUMN, STAT],
            scratch_shapes=[pltpu.VMEM((2 * len(keys), BS, STEP), jnp.bfloat16)] * 2,
        ),
        compiler_params=PARAMS,
        name="near_attention",
    )(lists, queries, *keys, *values)


def merge(polar, outs, stats):
    return pl.pallas_call(
        merge_kernel,
        out_shape=jax.ShapeDtypeStruct((TILE, D), jnp.bfloat16),
        grid_spec=pltpu.PrefetchScalarGridSpec(
            num_scalar_prefetch=1,
            grid=(D // STEP,),
            in_specs=[COLUMN] * 3 + [STAT] * 3,
            out_specs=COLUMN,
        ),
        compiler_params=PARAMS,
        name="merge",
    )(polar, *outs, *stats)


def local(queries, key_tokens, value_tokens, block_lists, band_rows):
    q = queries.reshape(TILE, D)
    k = key_tokens.reshape(TILE, D)
    v = value_tokens.reshape(TILE, D)
    lists = block_lists.reshape(2 * NB)
    lat_at = lax.axis_index("lat")
    is_polar = (lat_at == 0) | (lat_at == lax.axis_size("lat") - 1)
    polar = is_polar.astype(jnp.int32).reshape(1)
    fence = lax.optimization_barrier

    picked = jnp.where(is_polar, k[band_rows[0]], core_move(v[band_rows[0]], False))
    k_west, k_east = step_lon(k, 1), step_lon(k, -1)
    k_west, k_east, v_sent = fence((k_west, k_east, v))
    v_west, v_east = step_lon(v_sent, 1), step_lon(v_sent, -1)
    k_west, k_east, v_west, v_east = fence((k_west, k_east, v_west, v_east))
    k_west2, k_east2 = step_lon(k_west, 1), step_lon(k_east, -1)
    v_west, v_east, k_west2, k_east2 = fence((v_west, v_east, k_west2, k_east2))
    v_west2, v_east2 = step_lon(v_west, 1), step_lon(v_east, -1)

    q_other = polar_move(q, across_x)
    line = share(picked, Z_LINES)
    south, north = move(line, along_y(1)), move(line, along_y(-1))
    half = TILE // 4
    z_at = lax.axis_index("lon") & 7
    first = jnp.where(z_at == 0, north[:half], south[:half])
    second = jnp.where(z_at == 7, south[half:], north[half:])
    south2 = move(first, lambda lon: along_y(1 if lon & 7 else -1)(lon))
    north2 = move(second, lambda lon: along_y(1 if lon & 7 == 7 else -1)(lon))
    band = [line, south, north, south2, north2]
    band_v = [core_move(part, True) for part in band]
    own_out, other_out, own_stat, other_stat = band_attention(polar, q, q_other, band, band_v)
    near_out, near_stat = near_attention(
        lists,
        q,
        (k_west2, k_west, k, k_east, k_east2),
        (v_west2, v_west, v, v_east, v_east2),
    )
    other_out, other_stat = polar_move(other_out, across_x), polar_move(other_stat, across_x)
    near_out, other_out, other_stat = fence((near_out, other_out, other_stat))
    out = merge(
        polar, (near_out, own_out, other_out), (near_stat, own_stat, other_stat)
    )
    return out.reshape(queries.shape)


def solution(mesh):
    return jax.shard_map(
        local,
        mesh=mesh,
        in_specs=(
            P("lat", "lon", None),
            P("lat", "lon", None),
            P("lat", "lon", None),
            P("lat", "lon", None),
            P("lat", "lon"),
        ),
        out_specs=P("lat", "lon", None),
        check_vma=False,
    )
```

```python
import jax
import jax.numpy as jnp
from jax import lax
from jax.experimental import pallas as pl
from jax.experimental.pallas import tpu as pltpu
from jax.sharding import PartitionSpec as P

H = 24
HD = 64
BS = 128
TILE = 256
D = 1536
PAIR = 2 * HD
NB = 8
CAND = 10
N_LON = 64
LOG2E = 1.4426950408889634
STEP = 3 * PAIR
TOTALS = 32
POLAR_LATS = (0, 3)
POLAR_LATS = (0, 3)


def step_lon(value, steps):
    pairs = [(source, (source + steps) % N_LON) for source in range(N_LON)]
    return lax.ppermute(value, "lon", pairs)


def core_move(value, toward_polar):
    pairs = [
        (side, home) if toward_polar else (home, side)
        for polar_lat, side_lat in ((0, 1), (3, 2))
        for home, side in (
            (polar_lat * N_LON + lon, side_lat * N_LON + lon) for lon in range(N_LON)
        )
    ]
    return lax.ppermute(value, ("lat", "lon"), pairs)


def share(value, groups):
    copies = jnp.broadcast_to(value, (8,) + value.shape)
    got = lax.all_to_all(copies, "lon", 0, 0, axis_index_groups=groups)
    return got.reshape((-1,) + value.shape[1:])


Z_LINES = [[first + z for z in range(8)] for first in range(0, N_LON, 8)]


def move(value, target_of):
    return lax.ppermute(value, "lon", [(lon, target_of(lon)) for lon in range(N_LON)])


def polar_move(value, target_of):
    pairs = [
        (lat * N_LON + lon, lat * N_LON + target_of(lon))
        for lat in POLAR_LATS
        for lon in range(N_LON)
    ]
    return lax.ppermute(value, ("lat", "lon"), pairs)


def along_y(steps):
    return lambda lon: (lon & ~24) | ((lon + 8 * steps) & 24)


def across_x(lon):
    return lon ^ 32


def low_lanes():
    return lax.broadcasted_iota(jnp.int32, (BS, PAIR), 1) < HD


def attend(q, keys, values, low):
    q = q * jnp.bfloat16(HD ** -0.5)
    zero = jnp.zeros_like(q)
    stacked = jnp.concatenate([jnp.where(low, q, zero), jnp.where(low, zero, q)], 0)
    keys, values = jnp.concatenate(keys, 0), jnp.concatenate(values, 0)
    scores = lax.dot_general(
        stacked, keys, (((1,), (1,)), ((), ())), preferred_element_type=jnp.float32
    )
    row_max = jnp.max(scores, axis=1, keepdims=True)
    weights = jnp.exp2((scores - row_max) * LOG2E).astype(jnp.bfloat16)
    wide = jnp.concatenate([values, jnp.ones_like(values)], 1)
    mixed = jnp.dot(weights, wide, preferred_element_type=jnp.float32)
    acc = jnp.where(low, mixed[:BS, :PAIR], mixed[BS:, :PAIR])
    total = jnp.where(low, mixed[:BS, PAIR:], mixed[BS:, PAIR:])
    return acc, total, row_max


def pack(stat, head, total, row_max):
    lane = lax.broadcasted_iota(jnp.int32, (BS, PAIR), 1)
    stat = jnp.where(lane == head, row_max[:BS], stat)
    stat = jnp.where(lane == head + 1, row_max[BS:], stat)
    stat = jnp.where(lane == head + TOTALS, total[:, :1], stat)
    return jnp.where(lane == head + 1 + TOTALS, total[:, HD:HD + 1], stat)


def band_kernel(polar_ref, q_own, q_other, *refs):
    band_k, band_v = refs[0:5], refs[5:10]
    outs, stats = refs[10:12], refs[12:14]
    at = pl.program_id(0)

    @pl.when(polar_ref[0] == 1)
    def _():
        low = low_lanes()
        for q_ref, out_ref, stat_ref in zip((q_own, q_other), outs, stats):
            for block in range(2):
                rows = pl.ds(block * BS, BS)
                stat = jnp.where(at == 0, 0.0, stat_ref[rows, :])
                for part in range(STEP // PAIR):
                    lanes = slice(part * PAIR, (part + 1) * PAIR)
                    acc, total, row_max = attend(
                        q_ref[rows, lanes],
                        [ref[:, lanes] for ref in band_k],
                        [ref[:, lanes] for ref in band_v],
                        low,
                    )
                    out_ref[rows, lanes] = (acc / total).astype(out_ref.dtype)
                    stat = pack(stat, 2 * (at * (STEP // PAIR) + part), total, row_max)
                stat_ref[rows, :] = stat


def near_kernel(lists_ref, *refs):
    q_ref, k_tiles, v_tiles = refs[0], refs[1:6], refs[6:11]
    out_ref, stat_ref, k_all, v_all = refs[11:]
    at = pl.program_id(0)
    for tile in range(5):
        for block in range(2):
            rows = pl.ds(block * BS, BS)
            k_all[2 * tile + block] = k_tiles[tile][rows, :]
            v_all[2 * tile + block] = v_tiles[tile][rows, :]
    low = low_lanes()
    for block in range(2):
        rows = pl.ds(block * BS, BS)
        stat = jnp.where(at == 0, 0.0, stat_ref[rows, :])
        picks = [lists_ref[block * NB + j] for j in range(NB)]
        for part in range(STEP // PAIR):
            lanes = slice(part * PAIR, (part + 1) * PAIR)
            acc, total, row_max = attend(
                q_ref[rows, lanes],
                [k_all[pick, :, lanes] for pick in picks],
                [v_all[pick, :, lanes] for pick in picks],
                low,
            )
            out_ref[rows, lanes] = acc / total
            stat = pack(stat, 2 * (at * (STEP // PAIR) + part), total, row_max)
        stat_ref[rows, :] = stat


def spread(share, at):
    high = share.astype(jnp.bfloat16)
    rest = share - high.astype(jnp.float32)
    middle = rest.astype(jnp.bfloat16)
    tail = (rest - middle.astype(jnp.float32)).astype(jnp.bfloat16)
    column = lax.broadcasted_iota(jnp.int32, (PAIR, STEP), 0)
    lane = lax.broadcasted_iota(jnp.int32, (PAIR, STEP), 1)
    select = jnp.where(column == at * (STEP // HD) + lane // HD, 1.0, 0.0).astype(jnp.bfloat16)
    pieces = jnp.concatenate([high, middle, tail], 1)
    return jnp.dot(
        pieces, jnp.concatenate([select] * 3, 0), preferred_element_type=jnp.float32
    )


def merge_kernel(polar_ref, near_ref, own_ref, other_ref, *refs):
    stats, out_ref = refs[0:3], refs[3]
    at = pl.program_id(0)

    @pl.when(polar_ref[0] == 1)
    def _():
        heads = lax.broadcasted_iota(jnp.int32, (TILE, PAIR), 1) < D // HD
        stat = [ref[...] for ref in stats]
        top = jnp.maximum(stat[0], jnp.maximum(stat[1], stat[2]))
        masses = [
            jnp.exp2((each - top) * LOG2E) * pltpu.roll(each, PAIR - TOTALS, 1) for each in stat
        ]
        whole = masses[0] + masses[1] + masses[2]
        result = None
        for mass, ref in zip(masses, (near_ref, own_ref, other_ref)):
            share = jnp.where(heads, mass / whole, 0.0)
            part = ref[...].astype(jnp.float32) * spread(share, at)
            result = part if result is None else result + part
        out_ref[...] = result.astype(out_ref.dtype)

    @pl.when(polar_ref[0] == 0)
    def _():
        out_ref[...] = near_ref[...].astype(out_ref.dtype)


COLUMN = pl.BlockSpec((TILE, STEP), lambda p, *_: (0, p))
STAT = pl.BlockSpec((TILE, PAIR), lambda p, *_: (0, 0))
PARAMS = pltpu.CompilerParams(vmem_limit_bytes=60 << 20)


def band_attention(polar, q_own, q_other, band_k, band_v):
    def polar_column(rows):
        return pl.BlockSpec((rows, STEP), lambda p, polar_ref: (0, p * polar_ref[0]))

    return pl.pallas_call(
        band_kernel,
        out_shape=[jax.ShapeDtypeStruct((TILE, D), jnp.bfloat16)] * 2
        + [jax.ShapeDtypeStruct((TILE, PAIR), jnp.float32)] * 2,
        grid_spec=pltpu.PrefetchScalarGridSpec(
            num_scalar_prefetch=1,
            grid=(D // STEP,),
            in_specs=[polar_column(TILE)] * 2
            + [polar_column(part.shape[0]) for part in (*band_k, *band_v)],
            out_specs=[COLUMN] * 2 + [STAT] * 2,
        ),
        compiler_params=PARAMS,
        cost_estimate=pl.CostEstimate(
            flops=6 * 10 ** 10, transcendentals=0, bytes_accessed=TILE * D * 30
        ),
        name="band_attention",
    )(polar, q_own, q_other, *band_k, *band_v)


def near_attention(lists, queries, keys, values):
    return pl.pallas_call(
        near_kernel,
        out_shape=[
            jax.ShapeDtypeStruct((TILE, D), jnp.float32),
            jax.ShapeDtypeStruct((TILE, PAIR), jnp.float32),
        ],
        grid_spec=pltpu.PrefetchScalarGridSpec(
            num_scalar_prefetch=1,
            grid=(D // STEP,),
            in_specs=[COLUMN] * 11,
            out_specs=[COLUMN, STAT],
            scratch_shapes=[pltpu.VMEM((2 * len(keys), BS, STEP), jnp.bfloat16)] * 2,
        ),
        compiler_params=PARAMS,
        name="near_attention",
    )(lists, queries, *keys, *values)


def merge(polar, outs, stats):
    return pl.pallas_call(
        merge_kernel,
        out_shape=jax.ShapeDtypeStruct((TILE, D), jnp.bfloat16),
        grid_spec=pltpu.PrefetchScalarGridSpec(
            num_scalar_prefetch=1,
            grid=(D // STEP,),
            in_specs=[COLUMN] * 3 + [STAT] * 3,
            out_specs=COLUMN,
        ),
        compiler_params=PARAMS,
        name="merge",
    )(polar, *outs, *stats)


def local(queries, key_tokens, value_tokens, block_lists, band_rows):
    q = queries.reshape(TILE, D)
    k = key_tokens.reshape(TILE, D)
    v = value_tokens.reshape(TILE, D)
    lists = block_lists.reshape(2 * NB)
    lat_at = lax.axis_index("lat")
    is_polar = (lat_at == 0) | (lat_at == lax.axis_size("lat") - 1)
    polar = is_polar.astype(jnp.int32).reshape(1)
    fence = lax.optimization_barrier

    picked = jnp.where(is_polar, k[band_rows[0]], core_move(v[band_rows[0]], False))
    k_west, k_east = step_lon(k, 1), step_lon(k, -1)
    k_west, k_east, v_sent = fence((k_west, k_east, v))
    v_west, v_east = step_lon(v_sent, 1), step_lon(v_sent, -1)
    k_west, k_east, v_west, v_east = fence((k_west, k_east, v_west, v_east))
    k_west2, k_east2 = step_lon(k_west, 1), step_lon(k_east, -1)
    v_west, v_east, k_west2, k_east2 = fence((v_west, v_east, k_west2, k_east2))
    v_west2, v_east2 = step_lon(v_west, 1), step_lon(v_east, -1)

    q_other = polar_move(q, across_x)
    line = share(picked, Z_LINES)
    south, north = move(line, along_y(1)), move(line, along_y(-1))
    half = TILE // 4
    z_at = lax.axis_index("lon") & 7
    first = jnp.where(z_at == 0, north[:half], south[:half])
    second = jnp.where(z_at == 7, south[half:], north[half:])
    south2 = move(first, lambda lon: along_y(1 if lon & 7 else -1)(lon))
    north2 = move(second, lambda lon: along_y(1 if lon & 7 == 7 else -1)(lon))
    band = [line, south, north, south2, north2]
    band_v = [core_move(part, True) for part in band]
    own_out, other_out, own_stat, other_stat = band_attention(polar, q, q_other, band, band_v)
    near_out, near_stat = near_attention(
        lists,
        q,
        (k_west2, k_west, k, k_east, k_east2),
        (v_west2, v_west, v, v_east, v_east2),
    )
    other_out, other_stat = polar_move(other_out, across_x), polar_move(other_stat, across_x)
    near_out, other_out, other_stat = fence((near_out, other_out, other_stat))
    out = merge(
        polar, (near_out, own_out, other_out), (near_stat, own_stat, other_stat)
    )
    return out.reshape(queries.shape)


def solution(mesh):
    return jax.shard_map(
        local,
        mesh=mesh,
        in_specs=(
            P("lat", "lon", None),
            P("lat", "lon", None),
            P("lat", "lon", None),
            P("lat", "lon", None),
            P("lat", "lon"),
        ),
        out_specs=P("lat", "lon", None),
        check_vma=False,
    )
```

```python
import jax
import jax.numpy as jnp
from jax import lax
from jax.experimental import pallas as pl
from jax.experimental.pallas import tpu as pltpu
from jax.sharding import PartitionSpec as P

H = 24
HD = 64
BS = 128
TILE = 256
D = 1536
PAIR = 2 * HD
NB = 8
CAND = 10
N_LON = 64
LOG2E = 1.4426950408889634
STEP = 4 * PAIR
TOTALS = 32
POLAR_LATS = (0, 3)
POLAR_LATS = (0, 3)


def step_lon(value, steps):
    pairs = [(source, (source + steps) % N_LON) for source in range(N_LON)]
    return lax.ppermute(value, "lon", pairs)


def core_move(value, toward_polar):
    pairs = [
        (side, home) if toward_polar else (home, side)
        for polar_lat, side_lat in ((0, 1), (3, 2))
        for home, side in (
            (polar_lat * N_LON + lon, side_lat * N_LON + lon) for lon in range(N_LON)
        )
    ]
    return lax.ppermute(value, ("lat", "lon"), pairs)


def share(value, groups):
    copies = jnp.broadcast_to(value, (8,) + value.shape)
    got = lax.all_to_all(copies, "lon", 0, 0, axis_index_groups=groups)
    return got.reshape((-1,) + value.shape[1:])


Z_LINES = [[first + z for z in range(8)] for first in range(0, N_LON, 8)]


def move(value, target_of):
    return lax.ppermute(value, "lon", [(lon, target_of(lon)) for lon in range(N_LON)])


def polar_move(value, target_of):
    pairs = [
        (lat * N_LON + lon, lat * N_LON + target_of(lon))
        for lat in POLAR_LATS
        for lon in range(N_LON)
    ]
    return lax.ppermute(value, ("lat", "lon"), pairs)


def along_y(steps):
    return lambda lon: (lon & ~24) | ((lon + 8 * steps) & 24)


def across_x(lon):
    return lon ^ 32


def low_lanes():
    return lax.broadcasted_iota(jnp.int32, (BS, PAIR), 1) < HD


def attend(q, keys, values, low):
    q = q * jnp.bfloat16(HD ** -0.5)
    zero = jnp.zeros_like(q)
    stacked = jnp.concatenate([jnp.where(low, q, zero), jnp.where(low, zero, q)], 0)
    keys, values = jnp.concatenate(keys, 0), jnp.concatenate(values, 0)
    scores = lax.dot_general(
        stacked, keys, (((1,), (1,)), ((), ())), preferred_element_type=jnp.float32
    )
    row_max = jnp.max(scores, axis=1, keepdims=True)
    weights = jnp.exp2((scores - row_max) * LOG2E).astype(jnp.bfloat16)
    wide = jnp.concatenate([values, jnp.ones_like(values)], 1)
    mixed = jnp.dot(weights, wide, preferred_element_type=jnp.float32)
    acc = jnp.where(low, mixed[:BS, :PAIR], mixed[BS:, :PAIR])
    total = jnp.where(low, mixed[:BS, PAIR:], mixed[BS:, PAIR:])
    return acc, total, row_max


def pack(stat, head, total, row_max):
    lane = lax.broadcasted_iota(jnp.int32, (BS, PAIR), 1)
    stat = jnp.where(lane == head, row_max[:BS], stat)
    stat = jnp.where(lane == head + 1, row_max[BS:], stat)
    stat = jnp.where(lane == head + TOTALS, total[:, :1], stat)
    return jnp.where(lane == head + 1 + TOTALS, total[:, HD:HD + 1], stat)


def band_kernel(polar_ref, q_own, q_other, *refs):
    band_k, band_v = refs[0:5], refs[5:10]
    outs, stats = refs[10:12], refs[12:14]
    at = pl.program_id(0)

    @pl.when(polar_ref[0] == 1)
    def _():
        low = low_lanes()
        for q_ref, out_ref, stat_ref in zip((q_own, q_other), outs, stats):
            for block in range(2):
                rows = pl.ds(block * BS, BS)
                stat = jnp.where(at == 0, 0.0, stat_ref[rows, :])
                for part in range(STEP // PAIR):
                    lanes = slice(part * PAIR, (part + 1) * PAIR)
                    acc, total, row_max = attend(
                        q_ref[rows, lanes],
                        [ref[:, lanes] for ref in band_k],
                        [ref[:, lanes] for ref in band_v],
                        low,
                    )
                    out_ref[rows, lanes] = (acc / total).astype(out_ref.dtype)
                    stat = pack(stat, 2 * (at * (STEP // PAIR) + part), total, row_max)
                stat_ref[rows, :] = stat


def near_kernel(lists_ref, *refs):
    q_ref, k_tiles, v_tiles = refs[0], refs[1:6], refs[6:11]
    out_ref, stat_ref, k_all, v_all = refs[11:]
    at = pl.program_id(0)
    for tile in range(5):
        for block in range(2):
            rows = pl.ds(block * BS, BS)
            k_all[2 * tile + block] = k_tiles[tile][rows, :]
            v_all[2 * tile + block] = v_tiles[tile][rows, :]
    low = low_lanes()
    for block in range(2):
        rows = pl.ds(block * BS, BS)
        stat = jnp.where(at == 0, 0.0, stat_ref[rows, :])
        picks = [lists_ref[block * NB + j] for j in range(NB)]
        for part in range(STEP // PAIR):
            lanes = slice(part * PAIR, (part + 1) * PAIR)
            acc, total, row_max = attend(
                q_ref[rows, lanes],
                [k_all[pick, :, lanes] for pick in picks],
                [v_all[pick, :, lanes] for pick in picks],
                low,
            )
            out_ref[rows, lanes] = acc / total
            stat = pack(stat, 2 * (at * (STEP // PAIR) + part), total, row_max)
        stat_ref[rows, :] = stat


def spread(share, at):
    high = share.astype(jnp.bfloat16)
    rest = share - high.astype(jnp.float32)
    middle = rest.astype(jnp.bfloat16)
    tail = (rest - middle.astype(jnp.float32)).astype(jnp.bfloat16)
    column = lax.broadcasted_iota(jnp.int32, (PAIR, STEP), 0)
    lane = lax.broadcasted_iota(jnp.int32, (PAIR, STEP), 1)
    select = jnp.where(column == at * (STEP // HD) + lane // HD, 1.0, 0.0).astype(jnp.bfloat16)
    pieces = jnp.concatenate([high, middle, tail], 1)
    return jnp.dot(
        pieces, jnp.concatenate([select] * 3, 0), preferred_element_type=jnp.float32
    )


def merge_kernel(polar_ref, near_ref, own_ref, other_ref, *refs):
    stats, out_ref = refs[0:3], refs[3]
    at = pl.program_id(0)

    @pl.when(polar_ref[0] == 1)
    def _():
        heads = lax.broadcasted_iota(jnp.int32, (TILE, PAIR), 1) < D // HD
        stat = [ref[...] for ref in stats]
        top = jnp.maximum(stat[0], jnp.maximum(stat[1], stat[2]))
        masses = [
            jnp.exp2((each - top) * LOG2E) * pltpu.roll(each, PAIR - TOTALS, 1) for each in stat
        ]
        whole = masses[0] + masses[1] + masses[2]
        result = None
        for mass, ref in zip(masses, (near_ref, own_ref, other_ref)):
            share = jnp.where(heads, mass / whole, 0.0)
            part = ref[...].astype(jnp.float32) * spread(share, at)
            result = part if result is None else result + part
        out_ref[...] = result.astype(out_ref.dtype)

    @pl.when(polar_ref[0] == 0)
    def _():
        out_ref[...] = near_ref[...].astype(out_ref.dtype)


COLUMN = pl.BlockSpec((TILE, STEP), lambda p, *_: (0, p))
STAT = pl.BlockSpec((TILE, PAIR), lambda p, *_: (0, 0))
PARAMS = pltpu.CompilerParams(vmem_limit_bytes=60 << 20)


def band_attention(polar, q_own, q_other, band_k, band_v):
    def polar_column(rows):
        return pl.BlockSpec((rows, STEP), lambda p, polar_ref: (0, p * polar_ref[0]))

    return pl.pallas_call(
        band_kernel,
        out_shape=[jax.ShapeDtypeStruct((TILE, D), jnp.bfloat16)] * 2
        + [jax.ShapeDtypeStruct((TILE, PAIR), jnp.float32)] * 2,
        grid_spec=pltpu.PrefetchScalarGridSpec(
            num_scalar_prefetch=1,
            grid=(D // STEP,),
            in_specs=[polar_column(TILE)] * 2
            + [polar_column(part.shape[0]) for part in (*band_k, *band_v)],
            out_specs=[COLUMN] * 2 + [STAT] * 2,
        ),
        compiler_params=PARAMS,
        cost_estimate=pl.CostEstimate(
            flops=6 * 10 ** 10, transcendentals=0, bytes_accessed=TILE * D * 30
        ),
        name="band_attention",
    )(polar, q_own, q_other, *band_k, *band_v)


def near_attention(lists, queries, keys, values):
    return pl.pallas_call(
        near_kernel,
        out_shape=[
            jax.ShapeDtypeStruct((TILE, D), jnp.float32),
            jax.ShapeDtypeStruct((TILE, PAIR), jnp.float32),
        ],
        grid_spec=pltpu.PrefetchScalarGridSpec(
            num_scalar_prefetch=1,
            grid=(D // STEP,),
            in_specs=[COLUMN] * 11,
            out_specs=[COLUMN, STAT],
            scratch_shapes=[pltpu.VMEM((2 * len(keys), BS, STEP), jnp.bfloat16)] * 2,
        ),
        compiler_params=PARAMS,
        name="near_attention",
    )(lists, queries, *keys, *values)


def merge(polar, outs, stats):
    return pl.pallas_call(
        merge_kernel,
        out_shape=jax.ShapeDtypeStruct((TILE, D), jnp.bfloat16),
        grid_spec=pltpu.PrefetchScalarGridSpec(
            num_scalar_prefetch=1,
            grid=(D // STEP,),
            in_specs=[COLUMN] * 3 + [STAT] * 3,
            out_specs=COLUMN,
        ),
        compiler_params=PARAMS,
        name="merge",
    )(polar, *outs, *stats)


def local(queries, key_tokens, value_tokens, block_lists, band_rows):
    q = queries.reshape(TILE, D)
    k = key_tokens.reshape(TILE, D)
    v = value_tokens.reshape(TILE, D)
    lists = block_lists.reshape(2 * NB)
    lat_at = lax.axis_index("lat")
    is_polar = (lat_at == 0) | (lat_at == lax.axis_size("lat") - 1)
    polar = is_polar.astype(jnp.int32).reshape(1)
    fence = lax.optimization_barrier

    picked = jnp.where(is_polar, k[band_rows[0]], core_move(v[band_rows[0]], False))
    k_west, k_east = step_lon(k, 1), step_lon(k, -1)
    k_west, k_east, v_sent = fence((k_west, k_east, v))
    v_west, v_east = step_lon(v_sent, 1), step_lon(v_sent, -1)
    k_west, k_east, v_west, v_east = fence((k_west, k_east, v_west, v_east))
    k_west2, k_east2 = step_lon(k_west, 1), step_lon(k_east, -1)
    v_west, v_east, k_west2, k_east2 = fence((v_west, v_east, k_west2, k_east2))
    v_west2, v_east2 = step_lon(v_west, 1), step_lon(v_east, -1)

    q_other = polar_move(q, across_x)
    line = share(picked, Z_LINES)
    south, north = move(line, along_y(1)), move(line, along_y(-1))
    half = TILE // 4
    z_at = lax.axis_index("lon") & 7
    first = jnp.where(z_at == 0, north[:half], south[:half])
    second = jnp.where(z_at == 7, south[half:], north[half:])
    south2 = move(first, lambda lon: along_y(1 if lon & 7 else -1)(lon))
    north2 = move(second, lambda lon: along_y(1 if lon & 7 == 7 else -1)(lon))
    band = [line, south, north, south2, north2]
    band_v = [core_move(part, True) for part in band]
    own_out, other_out, own_stat, other_stat = band_attention(polar, q, q_other, band, band_v)
    near_out, near_stat = near_attention(
        lists,
        q,
        (k_west2, k_west, k, k_east, k_east2),
        (v_west2, v_west, v, v_east, v_east2),
    )
    other_out, other_stat = polar_move(other_out, across_x), polar_move(other_stat, across_x)
    near_out, other_out, other_stat = fence((near_out, other_out, other_stat))
    out = merge(
        polar, (near_out, own_out, other_out), (near_stat, own_stat, other_stat)
    )
    return out.reshape(queries.shape)


def solution(mesh):
    return jax.shard_map(
        local,
        mesh=mesh,
        in_specs=(
            P("lat", "lon", None),
            P("lat", "lon", None),
            P("lat", "lon", None),
            P("lat", "lon", None),
            P("lat", "lon"),
        ),
        out_specs=P("lat", "lon", None),
        check_vma=False,
    )
```
